256 devices in a mesh: chain: 2 (over core), leaf: 16 (over y, x), head: 8 (over z).
Axes of the slice: x: 4, y: 4, z: 8, core: 2. Of those that a mesh axis runs over, the one named last changes fastest.
Arguments:
- query_in: bfloat16 [16384, 16, 128], P(('chain', 'leaf'), 'head'), may hold values from -6 to 6
- key_in: bfloat16 [16384, 16, 128], P(('chain', 'leaf'), 'head'), may hold values from -120 to 120
- value_in: bfloat16 [16384, 16, 128], P(('chain', 'leaf'), 'head'), may hold values from -6 to 6
- gate_in: bfloat16 [16384, 16, 128], P(('chain', 'leaf'), 'head'), may hold values from -6 to 6
- write_strength: float32 [16, 16384], P('head', ('chain', 'leaf')), as said below
- log_decay: float32 [16, 16384], P('head', ('chain', 'leaf')), as said below
- doc_resets: int32 [256], P(('chain', 'leaf')), may hold values from 0 to 1, as said below
- conv_weight: float32 [3, 4, 16, 128], P(None, None, 'head'), may hold values from -3 to 3
- output_norm_gain: float32 [128], replicated, may hold values from 0.25 to 1.75
- output_projection_weight: bfloat16 [2048, 4096], P(None, 'head'), may hold values from -0.125 to 0.125
Outputs:
- mixed: bfloat16 [16384, 4096], P(('chain', 'leaf'), 'head')
The draws below stay inside these ranges and needn't reach their ends.
Inputs may be any that keep to these rules, and one draw needn't show every extreme that they name: `write_strength`: strictly positive. `log_decay`: strictly negative. `doc_resets`: at least one block of every draw starts a document.
All inputs are finite; a program needn't handle non-finite values.
Results may differ from the reference program's by a relative error of at most 0.0064.
Values may be sent and summed in bfloat16 or wider, within the bound.
A program may use at most 64 MiB of HBM per device.

```python
import jax
import jax.numpy as jnp
from jax import lax

H = 16
DK = 128
DV = 128
D = 4096
BLOCK = 64
KCONV = 4
TOK_DEV = 512
TOKENS = 16384
NBLOCK = 256


def head_kinds(key):
    picker = jax.random.fold_in(key, 11)
    return jax.random.randint(picker, (H,), 0, 2) > 0


def draw_key_in(key, part):
    ladder = jnp.broadcast_to(jnp.arange(DK, dtype=jnp.int32), (H, DK))
    ranking = jax.random.permutation(jax.random.fold_in(key, 41), ladder, axis=1, independent=True)
    channel_scale = 30.0 ** (ranking.astype(jnp.float32) / (DK - 1))
    unscaled = jnp.clip(jax.random.normal(jax.random.fold_in(key, 42), (TOKENS, H, DK), jnp.float32), -4.0, 4.0)
    return (unscaled * channel_scale[None, :, :]).astype(jnp.bfloat16)


def draw_log_decay(key, part):
    lagging_version = head_kinds(key)
    rough = jax.random.uniform(jax.random.fold_in(key, 1), (H, TOKENS), jnp.float32, 0.5, 1.5)
    segment = jax.random.uniform(jax.random.fold_in(key, 2), (H, TOKENS // TOK_DEV, 1), jnp.float32, 0.5, 1.5)
    segment = jnp.broadcast_to(segment, (H, TOKENS // TOK_DEV, TOK_DEV)).reshape(H, TOKENS)
    fast_scale = jax.random.uniform(jax.random.fold_in(key, 3), (H, 1), jnp.float32, 20.0, 50.0)
    slow_scale = jax.random.uniform(jax.random.fold_in(key, 4), (H, 1), jnp.float32, 0.1, 0.5)
    rapid_fraction = -rough * segment / fast_scale
    leisurely_fraction = -rough * segment * slow_scale / TOKENS
    spots = jax.random.randint(jax.random.fold_in(key, 5), (H, 2), 0, TOKENS)
    objective_scores = jax.random.uniform(jax.random.fold_in(key, 6), (H, 2), jnp.float32, 0.2, 0.4)
    positions = jnp.arange(TOKENS, dtype=jnp.int32)
    hit_markers = positions[None, :, None] == spots[:, None, :]
    clustered_sets = jnp.sum(jnp.where(hit_markers, jnp.log(1.0 - objective_scores)[:, None, :], 0.0), axis=-1)
    return jnp.where(lagging_version[:, None], leisurely_fraction, rapid_fraction) + clustered_sets


def draw_write_strength(key, part):
    lagging_version = head_kinds(key)
    rough = jax.random.uniform(jax.random.fold_in(key, 21), (H, TOKENS), jnp.float32, 0.5, 1.5)
    fast_level = jax.random.uniform(jax.random.fold_in(key, 22), (H, 1), jnp.float32, 0.3, 0.65)
    slow_level = jax.random.uniform(jax.random.fold_in(key, 23), (H, 1), jnp.float32, 0.1, 0.3)
    slow_factor = min(0.5, 64.0 * DK / TOKENS)
    rapid_fraction = jnp.minimum(fast_level * rough, 1.0)
    leisurely_fraction = jnp.minimum(slow_level * rough * slow_factor, 1.0)
    return jnp.where(lagging_version[:, None], leisurely_fraction, rapid_fraction)


def draw_doc_resets(key, part):
    flagged = jax.random.randint(jax.random.fold_in(key, 31), (NBLOCK,), 0, 256) == 0
    forced = jax.random.randint(jax.random.fold_in(key, 32), (), 1, NBLOCK)
    marked = flagged | (jnp.arange(NBLOCK, dtype=jnp.int32) == forced)
    return marked.astype(jnp.int32)


def block_levels(key, shape, shards, least, largest):
    def one(dim, shards_of):
        draws = jax.random.uniform(jax.random.fold_in(jax.random.fold_in(key, 6), dim), (shards_of,), jnp.float32, least / len(shards), largest / len(shards))
        return jnp.repeat(jnp.exp(draws), shape[dim] // shards_of).reshape((-1,) + (1,) * (len(shape) - dim - 1))

    loudness = one(*shards[0])
    for cut in shards[1:]:
        loudness = loudness * one(*cut)
    return loudness


def bell_draw(key, dims, deviation, most, pieces=(), kind=jnp.bfloat16):
    level = block_levels(key, dims, pieces, -0.22, 0.18) if pieces else 1.0
    result = jax.random.normal(key, dims, jnp.float32) * deviation * level
    return jnp.minimum(jnp.maximum(result, -most), most).astype(kind)


def setup_inputs(seed: int = 0) -> dict:
    streams_of = jax.random.split(jax.random.key(seed), 11)
    return {
        "query_in": bell_draw(streams_of[0], (TOKENS, H, DK), 1.0, 6.0, ((0, 32), (1, 8))),
        "key_in": draw_key_in(jax.random.fold_in(streams_of[10], 71), 0),
        "value_in": bell_draw(streams_of[2], (TOKENS, H, DV), 1.0, 6.0, ((0, 32), (1, 8))),
        "gate_in": bell_draw(streams_of[3], (TOKENS, H, DV), 1.0, 6.0, ((0, 32), (1, 8))),
        "write_strength": draw_write_strength(jax.random.fold_in(streams_of[10], 71), 0),
        "log_decay": draw_log_decay(jax.random.fold_in(streams_of[10], 71), 0),
        "doc_resets": draw_doc_resets(jax.random.fold_in(streams_of[10], 71), 0),
        "conv_weight": bell_draw(streams_of[7], (3, KCONV, H, DK), KCONV ** -0.5, 3.0, ((2, 8),), jnp.float32),
        "output_norm_gain": jnp.clip(1.0 + 0.15 * jax.random.normal(streams_of[8], (DV,), jnp.float32), 0.25, 1.75),
        "output_projection_weight": bell_draw(streams_of[9], (H * DV, D), (H * DV) ** -0.5, 0.125, ((1, 8),)),
    }


highest = lax.Precision.HIGHEST
epsilon = 1e-06

def unit_rows(matrix):
    return matrix / jnp.sqrt(lax.optimization_barrier(jnp.sum(matrix * matrix, axis=-1, keepdims=True)) + epsilon)

def causal_filter(signal, weights):
    kernel = weights.shape[0]
    length = signal.shape[0]
    padded = jnp.pad(signal.astype(jnp.float32), ((kernel - 1, 0), (0, 0), (0, 0)))
    running = weights[0] * padded[0:length]
    for offset in range(1, kernel):
        running = running + weights[offset] * padded[offset:offset + length]
    return jax.nn.silu(running)

def block_terms(query_unit, key_unit, value_act, strength, decays, keep_block):
    block_len = query_unit.shape[1]
    depth_k = key_unit.shape[2]
    value_width = value_act.shape[2]
    row_index = lax.broadcasted_iota(jnp.int32, (block_len, block_len), 0)
    col_index = lax.broadcasted_iota(jnp.int32, (block_len, block_len), 1)
    strict_mask = row_index > col_index
    causal_mask = row_index >= col_index
    cumulative = jnp.cumsum(decays, axis=-1)
    spread_log = cumulative[:, :, None] - cumulative[:, None, :]
    fading = jnp.where(causal_mask, jnp.exp(jnp.where(causal_mask, spread_log, 0.0)), 0.0)
    growth = jnp.exp(cumulative)
    query_float = query_unit.astype(jnp.float32)
    key_float = key_unit.astype(jnp.float32)
    value_float = value_act.astype(jnp.float32)
    key_gram = jnp.einsum('nte,nse->nts', key_float, key_float, precision=highest)
    query_gram = jnp.einsum('nte,nse->nts', query_float, key_float, precision=highest)
    lower = jnp.where(strict_mask, strength[:, :, None] * fading * key_gram, 0.0)
    mixing = fading * query_gram
    targets = jnp.concatenate([strength[:, :, None] * value_float, (strength * growth)[:, :, None] * key_float], axis=-1)
    solved = jax.scipy.linalg.solve_triangular(jnp.eye(block_len, dtype=jnp.float32) + lower, targets, lower=True, unit_diagonal=True)
    local_values = solved[..., :value_width]
    write_keys = solved[..., value_width:]
    tail_fade = jnp.exp(cumulative[:, -1:] - cumulative)
    decayed_addresses = tail_fade[:, :, None] * key_float
    key_eye = jnp.eye(depth_k, dtype=jnp.float32)
    keep_mat = keep_block[:, None, None]
    transition = keep_mat * (growth[:, -1, None, None] * key_eye - jnp.einsum('nce,ncf->nef', decayed_addresses, write_keys, precision=highest))
    addition = jnp.einsum('nce,ncf->nef', decayed_addresses, local_values, precision=highest)
    query_eff = keep_mat * (growth[:, :, None] * query_float - jnp.einsum('nts,nse->nte', mixing, write_keys, precision=highest))
    own_output = jnp.einsum('nts,nsf->ntf', mixing, local_values, precision=highest)
    return (transition, addition, query_eff, own_output)

def head_core(argument_arrays):
    query_head, key_head, value_head, strength, decays, keep_block = argument_arrays
    length = query_head.shape[0]
    blocks = length // BLOCK
    all_terms = block_terms(query_head.reshape(blocks, BLOCK, -1), key_head.reshape(blocks, BLOCK, -1), value_head.reshape(blocks, BLOCK, -1), strength.reshape(blocks, BLOCK), decays.reshape(blocks, BLOCK), keep_block)

    def advance(state, terms_now):
        transition, addition, query_eff, own_output = terms_now
        produced = jnp.dot(query_eff.astype(jnp.float32), state.astype(jnp.float32), precision=highest, preferred_element_type=jnp.float32) + own_output
        following = jnp.dot(transition.astype(jnp.float32), state.astype(jnp.float32), precision=highest, preferred_element_type=jnp.float32) + addition
        return (following, produced)
    initial = jnp.zeros((key_head.shape[1], value_head.shape[1]), jnp.float32)
    final_state, produced = lax.scan(advance, initial, all_terms)
    return produced.reshape(length, value_head.shape[1])

def reference(query_in, key_in, value_in, gate_in, write_strength, log_decay, doc_resets, conv_weight, output_norm_gain, output_projection_weight):
    query_conv = causal_filter(query_in, conv_weight[0])
    key_conv = causal_filter(key_in, conv_weight[1])
    value_conv = causal_filter(value_in, conv_weight[2])
    query_unit = (unit_rows(query_conv) * DK ** (-0.5)).astype(jnp.bfloat16)
    key_unit = unit_rows(key_conv).astype(jnp.bfloat16)
    value_act = value_conv.astype(jnp.bfloat16)
    keep_block = (1 - doc_resets).astype(jnp.float32)
    keep_heads = jnp.broadcast_to(keep_block, (H, keep_block.shape[0]))
    core = lax.map(head_core, (jnp.moveaxis(query_unit, 1, 0), jnp.moveaxis(key_unit, 1, 0), jnp.moveaxis(value_act, 1, 0), write_strength, log_decay, keep_heads))
    core = jnp.moveaxis(core, 0, 1)
    scale_rms = jnp.sqrt(lax.optimization_barrier(jnp.mean(core * core, axis=-1, keepdims=True)) + epsilon)
    normed = (core / scale_rms * output_norm_gain * jax.nn.silu(gate_in.astype(jnp.float32))).astype(jnp.bfloat16)
    flat = normed.reshape(normed.shape[0], H * DV)
    return jnp.dot(flat.astype(jnp.float32), output_projection_weight.astype(jnp.float32), preferred_element_type=jnp.float32).astype(jnp.bfloat16)
```

```python
import jax
import jax.numpy as jnp
from jax import lax
from jax.sharding import PartitionSpec as P

BLOCK = 64


highest = lax.Precision.HIGHEST
epsilon = 1e-06
SEQ = ("chain", "leaf")


def mm(spec, a, b):
    return jnp.einsum(spec, a, b, precision=highest, preferred_element_type=jnp.float32)


def from_behind(value, axis, steps):
    count = lax.axis_size(axis)
    initial, last = (max(0, -steps), min(count, count - steps))
    return lax.ppermute(value, axis, [(source, source + steps) for source in range(initial, last)])


def unit_rows(matrix):
    return matrix / jnp.sqrt(jnp.sum(matrix * matrix, axis=-1, keepdims=True) + epsilon)


def causal_filter(signal, rim_rows, weights):
    kernel = weights.shape[0]
    length = signal.shape[0]
    padded = jnp.concatenate([rim_rows, signal], axis=0)
    running = weights[0] * padded[0:length]
    for offset in range(1, kernel):
        running = running + weights[offset] * padded[offset : offset + length]
    return jax.nn.silu(running)


def unit_lower_inverse(lower):
    size = lower.shape[-1]
    row = lax.broadcasted_iota(jnp.int32, (size, size), 0)
    col = lax.broadcasted_iota(jnp.int32, (size, size), 1)
    inverse = jnp.broadcast_to(jnp.eye(size, dtype=jnp.float32), lower.shape)
    span = 1
    while span < size:
        pick = ((row // (2 * span)) == (col // (2 * span))) & ((row // span) % 2 == 1) & (
            (col // span) % 2 == 0
        )
        coupling = jnp.where(pick, lower, 0.0)
        inverse = lax.optimization_barrier(inverse)
        inverse = inverse - mm("...ij,...jk->...ik", mm("...ij,...jk->...ik", inverse, coupling), inverse)
        span *= 2
    return inverse


def on_device(
    query_in,
    key_in,
    value_in,
    gate_in,
    write_strength,
    log_decay,
    doc_resets,
    conv_weight,
    output_norm_gain,
    output_projection_weight,
):
    length, head_count, depth_k = query_in.shape
    value_width = value_in.shape[2]
    kernel = conv_weight.shape[1]
    tail_rows = jnp.stack(
        [
            query_in[length - kernel + 1 :],
            key_in[length - kernel + 1 :],
            value_in[length - kernel + 1 :],
        ]
    )
    rim_rows = from_behind(tail_rows, SEQ, 1)
    query_conv = causal_filter(query_in, rim_rows[0], conv_weight[0])
    key_conv = causal_filter(key_in, rim_rows[1], conv_weight[1])
    value_conv = causal_filter(value_in, rim_rows[2], conv_weight[2])
    query_unit = (unit_rows(query_conv) * depth_k ** (-0.5)).astype(jnp.bfloat16)
    key_unit = unit_rows(key_conv).astype(jnp.bfloat16)
    value_act = value_conv.astype(jnp.bfloat16)
    blocks = length // BLOCK
    query_blk = query_unit.reshape(blocks, BLOCK, head_count, depth_k)
    key_blk = key_unit.reshape(blocks, BLOCK, head_count, depth_k)
    value_blk = value_act.reshape(blocks, BLOCK, head_count, value_width)
    key_gram = jnp.einsum("nthe,nshe->nhts", key_blk, key_blk, preferred_element_type=jnp.float32)
    query_gram = jnp.einsum(
        "nthe,nshe->nhts", query_blk, key_blk, preferred_element_type=jnp.float32
    )
    strength = write_strength.reshape(head_count, blocks, BLOCK).transpose(1, 0, 2)
    decays = log_decay.reshape(head_count, blocks, BLOCK).transpose(1, 0, 2)
    row_index = lax.broadcasted_iota(jnp.int32, (BLOCK, BLOCK), 0)
    col_index = lax.broadcasted_iota(jnp.int32, (BLOCK, BLOCK), 1)
    strict_mask = row_index > col_index
    causal_mask = row_index >= col_index
    cumulative = jnp.cumsum(decays, axis=-1)
    spread_log = cumulative[..., :, None] - cumulative[..., None, :]
    fading = jnp.where(causal_mask, jnp.exp(jnp.where(causal_mask, spread_log, 0.0)), 0.0)
    growth = jnp.exp(cumulative)
    lower = jnp.where(strict_mask, strength[..., :, None] * fading * key_gram, 0.0)
    mixing = fading * query_gram
    query_float = jnp.transpose(query_blk, (0, 2, 1, 3)).astype(jnp.float32)
    key_float = jnp.transpose(key_blk, (0, 2, 1, 3)).astype(jnp.float32)
    value_float = jnp.transpose(value_blk, (0, 2, 1, 3)).astype(jnp.float32)
    targets = jnp.concatenate(
        [strength[..., None] * value_float, (strength * growth)[..., None] * key_float], axis=-1
    )
    solved = mm("nhts,nhsf->nhtf", unit_lower_inverse(lower), targets)
    local_values = solved[..., :value_width]
    write_keys = solved[..., value_width:]
    tail_fade = jnp.exp(cumulative[..., -1:] - cumulative)
    decayed_addresses = tail_fade[..., None] * key_float
    key_eye = jnp.eye(depth_k, dtype=jnp.float32)
    keep_mat = (1 - doc_resets).astype(jnp.float32)[:, None, None, None]
    transition = keep_mat * (
        growth[..., -1, None, None] * key_eye
        - mm("nhce,nhcf->nhef", decayed_addresses, write_keys)
    )
    addition = mm("nhce,nhcf->nhef", decayed_addresses, local_values)
    query_eff = keep_mat * (
        growth[..., None] * query_float - mm("nhts,nhse->nhte", mixing, write_keys)
    )
    own_output = mm("nhts,nhsf->nhtf", mixing, local_values)
    carry = jnp.concatenate(
        [
            jnp.broadcast_to(key_eye, (head_count, depth_k, depth_k)),
            jnp.zeros((head_count, depth_k, value_width), jnp.float32),
        ],
        axis=-1,
    )
    starts = []
    for n in range(blocks):
        starts.append(carry)
        carry = mm("hij,hjk->hik", transition[n], carry)
        carry = carry.at[..., depth_k:].add(addition[n])
    starts = jnp.stack(starts)
    reach = mm("nhtd,nhde->nhte", query_eff, starts)
    partial_out = own_output + reach[..., depth_k:]
    reach_map = reach[..., :depth_k]
    device_trans = carry[..., :depth_k]
    device_state = carry[..., depth_k:]
    place = lax.axis_index(SEQ)
    count = lax.axis_size(SEQ)
    trans, state = device_trans, device_state
    stride = 1
    while stride < count:
        got_trans, got_state = from_behind((trans, state), SEQ, stride)
        has = place >= stride
        state = state + mm("hij,hjk->hik", trans, got_state)
        if stride * 2 < count:
            trans = jnp.where(has, mm("hij,hjk->hik", trans, got_trans), trans)
        stride *= 2
    incoming = from_behind(state, SEQ, 1)
    core = partial_out + mm("nhte,hef->nhtf", reach_map, incoming)
    core = jnp.transpose(core, (0, 2, 1, 3)).reshape(length, head_count, value_width)
    scale_rms = jnp.sqrt(jnp.mean(core * core, axis=-1, keepdims=True) + epsilon)
    normed = (
        core / scale_rms * output_norm_gain * jax.nn.silu(gate_in.astype(jnp.float32))
    ).astype(jnp.bfloat16)
    shard_piece = lax.all_gather(normed, "head", axis=1, tiled=True)
    count = shard_piece.shape[1]
    flat_piece = shard_piece.reshape(shard_piece.shape[0], count * value_width)
    mixed = jnp.dot(flat_piece, output_projection_weight, preferred_element_type=jnp.float32)
    return mixed.astype(jnp.bfloat16)


def solution(mesh):
    return jax.shard_map(
        on_device,
        mesh=mesh,
        in_specs=(
            P(("chain", "leaf"), "head", None),
            P(("chain", "leaf"), "head", None),
            P(("chain", "leaf"), "head", None),
            P(("chain", "leaf"), "head", None),
            P("head", ("chain", "leaf")),
            P("head", ("chain", "leaf")),
            P(("chain", "leaf")),
            P(None, None, "head", None),
            P(),
            P(None, "head"),
        ),
        out_specs=P(("chain", "leaf"), "head"),
        check_vma=False,
    )
```
